32 devices in a mesh: shard: 2 (over x), context: 4 (over y, core), tensor: 4 (over z).
Axes of the slice: x: 2, y: 2, z: 4, core: 2. Of those that a mesh axis runs over, the one named last changes fastest.
Arguments:
- hidden: float32 [2, 1024, 768], P('shard', 'context'), may hold values from -6 to 6
- enc_states: bfloat16 [2, 512, 768], P('shard', 'context'), may hold values from -6 to 6
- cotangent: float32 [2, 1024, 768], P('shard', 'context'), may hold values from -6 to 6
- segments: int32 [2, 1024], P('shard', 'context'), may hold values from 0 to 2, as said below
- positions: int32 [2, 1024], P('shard', 'context'), may hold values from 0 to 623, as said below
- enc_segments: int32 [2, 512], P('shard', 'context'), may hold values from 0 to 2, as said below
- doc_source: int32 [2, 3], P('shard'), may hold values from 0 to 2, each once within a row
- bucket_of: int32 [1024], replicated, may hold values from 0 to 31, as said below
- norm_self: float32 [768], replicated, may hold values from 0.5 to 1.5
- norm_cross: float32 [768], replicated, may hold values from 0.5 to 1.5
- norm_ffn: float32 [768], replicated, may hold values from 0.5 to 1.5
- bias_table: float32 [32, 12], P(None, 'tensor'), may hold values from -5 to 5
- w_q: bfloat16 [768, 768], P('shard', 'tensor'), may hold values from -0.0546875 to 0.0546875
- w_k: bfloat16 [768, 768], P('shard', 'tensor'), may hold values from -0.21875 to 0.21875
- w_v: bfloat16 [768, 768], P('shard', 'tensor'), may hold values from -0.21875 to 0.21875
- w_o: bfloat16 [768, 768], P('tensor', 'shard'), may hold values from -0.875 to 0.875
- c_q: bfloat16 [768, 768], P('shard', 'tensor'), may hold values from -0.0546875 to 0.0546875
- c_k: bfloat16 [768, 768], P('shard', 'tensor'), may hold values from -0.21875 to 0.21875
- c_v: bfloat16 [768, 768], P('shard', 'tensor'), may hold values from -0.21875 to 0.21875
- c_o: bfloat16 [768, 768], P('tensor', 'shard'), may hold values from -0.875 to 0.875
- w_gate: bfloat16 [768, 2048], P('shard', 'tensor'), may hold values from -0.21875 to 0.21875
- w_up: bfloat16 [768, 2048], P('shard', 'tensor'), may hold values from -0.21875 to 0.21875
- w_down: bfloat16 [2048, 768], P('tensor', 'shard'), may hold values from -0.125 to 0.125
Outputs:
- output: float32 [2, 1024, 768], P('shard', 'context')
- d_hidden: float32 [2, 1024, 768], P('shard', 'context')
- d_enc_states: float32 [2, 512, 768], P('shard', 'context')
- d_norm_self: float32 [768], replicated
- d_norm_cross: float32 [768], replicated
- d_norm_ffn: float32 [768], replicated
- d_bias_table: float32 [32, 12], P(None, 'tensor')
- d_w_q: float32 [768, 768], P('shard', 'tensor')
- d_w_k: float32 [768, 768], P('shard', 'tensor')
- d_w_v: float32 [768, 768], P('shard', 'tensor')
- d_w_o: float32 [768, 768], P('tensor', 'shard')
- d_c_q: float32 [768, 768], P('shard', 'tensor')
- d_c_k: float32 [768, 768], P('shard', 'tensor')
- d_c_v: float32 [768, 768], P('shard', 'tensor')
- d_c_o: float32 [768, 768], P('tensor', 'shard')
- d_w_gate: float32 [768, 2048], P('shard', 'tensor')
- d_w_up: float32 [768, 2048], P('shard', 'tensor')
- d_w_down: float32 [2048, 768], P('tensor', 'shard')
The draws below stay inside these ranges and needn't reach their ends.
Inputs may be any that keep to these rules, and one draw needn't show every extreme that they name: `segments`: in each sequence the document number starts at 0 and rises by one at each new document; there are exactly 3 documents, each a contiguous run of 200 tokens or more. positions count the tokens before this one in its document; some document is 624 tokens long. `enc_segments`: in each sequence the encoder segment number starts at 0 and rises by one at each new segment; exactly 3 segments, each a contiguous run of 64 encoder states or more. `doc_source`: each row is a permutation of 0 to 2. bucket_of is 0 at distance 0, never falls, and is 31 from distance 128 - 1 on.
All inputs are finite; a program needn't handle non-finite values.
Results may differ from the reference program's by a relative error of at most 0.023.
Values may be sent and summed in bfloat16 or wider, within the bound.
A program may use at most 128 MiB of HBM per device.

```python
import jax
import jax.numpy as jnp
from jax import lax

D = 768
H = 12
DH = 64
FF = 2048
NB = 32
BUCKET_SPAN = 128
L = 1024
ENC = 512
NDOC = 3
MIN_DOC = 200
ENC_MIN = 64
SEQS = 2


def layout(base_key, total_len, doc_count, least_len):
    spare_room = total_len - doc_count * least_len

    def single(seq_key, seq_index):
        drawn = jnp.sort(jax.random.permutation(seq_key, spare_room + doc_count - 1)[:doc_count - 1]).astype(jnp.int32)
        packed = jnp.arange(doc_count - 1, dtype=jnp.int32)
        chosen = jnp.where(seq_index == 0, packed, drawn).astype(jnp.int32)
        borders = jnp.concatenate([jnp.full((1,), -1, jnp.int32), chosen, jnp.full((1,), spare_room + doc_count - 1, jnp.int32)])
        doc_lengths = least_len + borders[1:] - borders[:-1] - 1
        doc_ends = jnp.cumsum(doc_lengths).astype(jnp.int32)
        index_row = jnp.arange(total_len, dtype=jnp.int32)
        segment_row = jnp.sum((index_row[:, None] >= doc_ends[None, :]).astype(jnp.int32), axis=1)
        document_offsets = doc_ends - doc_lengths
        start_of = jnp.sum(jnp.where(segment_row[:, None] == jnp.arange(doc_count, dtype=jnp.int32)[None, :], document_offsets[None, :], 0), axis=1)
        return (segment_row.astype(jnp.int32), (index_row - start_of).astype(jnp.int32))
    return jax.vmap(single)(jax.random.split(base_key, SEQS), jnp.arange(SEQS, dtype=jnp.int32))


def draw_segments(key, part):
    return layout(jax.random.fold_in(key, 11), L, NDOC, MIN_DOC)[0]


def draw_positions(key, part):
    return layout(jax.random.fold_in(key, 11), L, NDOC, MIN_DOC)[1]


def draw_enc_segments(key, part):
    return layout(jax.random.fold_in(key, 12), ENC, NDOC, ENC_MIN)[0]


def draw_bucket_of(key, part):
    chosen = jax.random.permutation(jax.random.fold_in(key, 13), BUCKET_SPAN - 1)[:NB - 1] + 1
    breaks = jnp.sort(chosen).astype(jnp.int32)
    distance = jnp.arange(L, dtype=jnp.int32)
    return jnp.sum((distance[:, None] >= breaks[None, :]).astype(jnp.int32), axis=1).astype(jnp.int32)


def block_levels(key, extent, pieces, smallest, top_value):
    def one(position, parts):
        draws = jax.random.uniform(jax.random.fold_in(jax.random.fold_in(key, 6), position), (parts,), jnp.float32, smallest / len(pieces), top_value / len(pieces))
        return jnp.repeat(jnp.exp(draws), extent[position] // parts).reshape((-1,) + (1,) * (len(extent) - position - 1))

    gain = one(*pieces[0])
    for cut in pieces[1:]:
        gain = gain * one(*cut)
    return gain


def bell_draw(own_key, extent, width, bound, pieces=(), held_as=jnp.bfloat16):
    gain = block_levels(own_key, extent, pieces, -0.22, 0.18) if pieces else 1.0
    array = jax.random.normal(own_key, extent, jnp.float32) * width * gain
    return jnp.minimum(jnp.maximum(array, -bound), bound).astype(held_as)


def setup_inputs(seed: int = 0) -> dict:
    key_list = jax.random.split(jax.random.key(seed), 24)
    hidden = bell_draw(key_list[0], (SEQS, L, D), 1.0, 6.0, ((0, 2), (1, 4)), jnp.float32)
    enc_states = bell_draw(key_list[1], (SEQS, ENC, D), 1.0, 6.0, ((0, 2), (1, 4)))
    cotangent = bell_draw(key_list[2], (SEQS, L, D), 1.0, 6.0, ((0, 2), (1, 4)), jnp.float32)
    segments = draw_segments(jax.random.fold_in(key_list[23], 71), 0)
    positions = draw_positions(jax.random.fold_in(key_list[23], 71), 0)
    enc_segments = draw_enc_segments(jax.random.fold_in(key_list[23], 71), 0)
    doc_source = jax.vmap(lambda own: jax.random.permutation(own, NDOC))(jax.random.split(key_list[6], SEQS)).reshape((SEQS, NDOC)).astype(jnp.int32)
    bucket_of = draw_bucket_of(jax.random.fold_in(key_list[23], 71), 0)
    norm_self = jnp.clip(1.0 + 0.1 * jax.random.normal(key_list[8], (D,), jnp.float32), 0.5, 1.5)
    norm_cross = jnp.clip(1.0 + 0.1 * jax.random.normal(key_list[9], (D,), jnp.float32), 0.5, 1.5)
    norm_ffn = jnp.clip(1.0 + 0.1 * jax.random.normal(key_list[10], (D,), jnp.float32), 0.5, 1.5)
    bias_table = bell_draw(key_list[11], (NB, H), 1.0, 5.0, ((1, 4),), jnp.float32)
    w_q = bell_draw(key_list[12], (D, H * DH), (D * DH // 4) ** -0.5, 0.0546875, ((0, 2), (1, 4)))
    w_k = bell_draw(key_list[13], (D, H * DH), D ** -0.5, 0.21875, ((0, 2), (1, 4)))
    w_v = bell_draw(key_list[14], (D, H * DH), D ** -0.5, 0.21875, ((0, 2), (1, 4)))
    w_o = bell_draw(key_list[15], (H * DH, D), (H * DH // 16) ** -0.5, 0.875, ((0, 4), (1, 2)))
    c_q = bell_draw(key_list[16], (D, H * DH), (D * DH // 4) ** -0.5, 0.0546875, ((0, 2), (1, 4)))
    c_k = bell_draw(key_list[17], (D, H * DH), D ** -0.5, 0.21875, ((0, 2), (1, 4)))
    c_v = bell_draw(key_list[18], (D, H * DH), D ** -0.5, 0.21875, ((0, 2), (1, 4)))
    c_o = bell_draw(key_list[19], (H * DH, D), (H * DH // 16) ** -0.5, 0.875, ((0, 4), (1, 2)))
    w_gate = bell_draw(key_list[20], (D, FF), D ** -0.5, 0.21875, ((0, 2), (1, 4)))
    w_up = bell_draw(key_list[21], (D, FF), D ** -0.5, 0.21875, ((0, 2), (1, 4)))
    w_down = bell_draw(key_list[22], (FF, D), FF ** -0.5, 0.125, ((0, 4), (1, 2)))
    return {"hidden": hidden, "enc_states": enc_states, "cotangent": cotangent, "segments": segments, "positions": positions, "enc_segments": enc_segments, "doc_source": doc_source, "bucket_of": bucket_of, "norm_self": norm_self, "norm_cross": norm_cross, "norm_ffn": norm_ffn, "bias_table": bias_table, "w_q": w_q, "w_k": w_k, "w_v": w_v, "w_o": w_o, "c_q": c_q, "c_k": c_k, "c_v": c_v, "c_o": c_o, "w_gate": w_gate, "w_up": w_up, "w_down": w_down}


@jax.custom_vjp
def low(v):
    return lax.optimization_barrier(v.astype(jnp.bfloat16)).astype(jnp.float32)

@jax.custom_vjp
def low_back(v):
    return v

def low_keep(v):
    return (low(v), None)

def low_pass(kept, grad):
    return (grad,)

def back_keep(v):
    return (v, None)

def back_low(kept, grad):
    return (low(grad),)
low.defvjp(low_keep, low_pass)
low_back.defvjp(back_keep, back_low)
PRECISION_FULL = lax.Precision.HIGHEST
EPSILON = 1e-06
MASKED = -1e+30

def project(input_rows, weight_matrix):
    return jnp.einsum('pnv,vu->pnu', input_rows, weight_matrix, precision=PRECISION_FULL)

def rms_gain(input_rows, gain_vec):
    return input_rows * lax.rsqrt(lax.optimization_barrier(jnp.mean(input_rows * input_rows, axis=-1, keepdims=True)) + EPSILON) * gain_vec

def attention(query, key_rows, value_rows, allowed, rel_bias):
    query_heads = query.reshape(query.shape[0], H, DH)
    key_heads = key_rows.reshape(key_rows.shape[0], H, DH)
    value_heads = value_rows.reshape(value_rows.shape[0], H, DH)
    scores = jnp.einsum('qhd,khd->hqk', query_heads, key_heads, precision=PRECISION_FULL)
    if rel_bias is not None:
        scores = scores + rel_bias
    scores = jnp.where(allowed[None], low_back(scores), MASKED)
    row_max = lax.optimization_barrier(jnp.max(scores, axis=2, keepdims=True))
    weights = jnp.exp(scores - row_max)
    probs = low(weights / lax.optimization_barrier(jnp.sum(weights, axis=2, keepdims=True)))
    mixed = jnp.einsum('hqk,khd->qhd', probs, value_heads, precision=PRECISION_FULL)
    return mixed.reshape(query.shape[0], H * DH)

def decoder_layer(params, labels):
    hidden, enc_states, norm_self, norm_cross, norm_ffn, bias_table, w_q, w_k, w_v, w_o, c_q, c_k, c_v, c_o, w_gate, w_up, w_down = params
    segments, positions, enc_segments, doc_source, bucket_of = labels
    normed_self = low(rms_gain(hidden, norm_self))
    queries = low(low_back(project(normed_self, w_q)))
    keys_self = low(low_back(project(normed_self, w_k)))
    values_self = low(low_back(project(normed_self, w_v)))

    def self_block(items):
        query, key_rows, value_rows, seg_row, pos_row = items
        allowed = (seg_row[:, None] == seg_row[None, :]) & (pos_row[None, :] <= pos_row[:, None])
        distance = jnp.clip(pos_row[:, None] - pos_row[None, :], 0, L - 1)
        rel_bias = jnp.transpose(bias_table[bucket_of[distance]], (2, 0, 1))
        return attention(query, key_rows, value_rows, allowed, rel_bias)
    self_mixed = low(low_back(lax.map(jax.checkpoint(self_block), (queries, keys_self, values_self, segments, positions))))
    after_self = hidden + low_back(project(self_mixed, w_o))
    normed_cross = low(rms_gain(after_self, norm_cross))
    cross_queries = low(low_back(project(normed_cross, c_q)))
    enc_keys = low(low_back(project(enc_states, c_k)))
    enc_values = low(low_back(project(enc_states, c_v)))

    def cross_block(items):
        query, key_rows, value_rows, seg_row, enc_row, doc_row = items
        target = doc_row[seg_row]
        allowed = enc_row[None, :] == target[:, None]
        return attention(query, key_rows, value_rows, allowed, None)
    cross_mixed = low(low_back(lax.map(jax.checkpoint(cross_block), (cross_queries, enc_keys, enc_values, segments, enc_segments, doc_source))))
    after_cross = after_self + low_back(project(cross_mixed, c_o))
    normed_ffn = low(rms_gain(after_cross, norm_ffn))
    gate_pre = low_back(project(normed_ffn, w_gate))
    up_pre = low_back(project(normed_ffn, w_up))
    units = low(jax.nn.gelu(gate_pre, approximate=True) * up_pre)
    return after_cross + low_back(project(units, w_down))

def reference(hidden, enc_states, cotangent, segments, positions, enc_segments, doc_source, bucket_of, norm_self, norm_cross, norm_ffn, bias_table, w_q, w_k, w_v, w_o, c_q, c_k, c_v, c_o, w_gate, w_up, w_down):
    params = (hidden, enc_states.astype(jnp.float32), norm_self, norm_cross, norm_ffn, bias_table, w_q.astype(jnp.float32), w_k.astype(jnp.float32), w_v.astype(jnp.float32), w_o.astype(jnp.float32), c_q.astype(jnp.float32), c_k.astype(jnp.float32), c_v.astype(jnp.float32), c_o.astype(jnp.float32), w_gate.astype(jnp.float32), w_up.astype(jnp.float32), w_down.astype(jnp.float32))
    labels = (segments, positions, enc_segments, doc_source, bucket_of)

    def forward(*params_in):
        return decoder_layer(params_in, labels)
    output, pull_back = jax.vjp(forward, *params)
    grads_all = pull_back(cotangent)
    return (output, grads_all[0], grads_all[1], grads_all[2], grads_all[3], grads_all[4], grads_all[5], grads_all[6], grads_all[7], grads_all[8], grads_all[9], grads_all[10], grads_all[11], grads_all[12], grads_all[13], grads_all[14], grads_all[15], grads_all[16])
```

```python
import functools
import itertools

import jax
import jax.numpy as jnp
from jax import lax
from jax.experimental import pallas as pl
from jax.experimental.pallas import tpu as pltpu
from jax.sharding import PartitionSpec as P

EPSILON = 1e-06
MASKED = -1e30
MESH = pl.DeviceIdType.MESH
BF16 = jnp.bfloat16
F32 = jnp.float32


def low(values):
    return values.astype(BF16)


def mm(left, right):
    return jnp.dot(left, right, preferred_element_type=F32)


def mm_tn(left, right):
    return lax.dot_general(
        left, right, (((0,), (0,)), ((), ())), preferred_element_type=F32
    )


def mm_nt(left, right):
    return lax.dot_general(
        left, right, (((1,), (1,)), ((), ())), preferred_element_type=F32
    )


def vmem():
    return pl.BlockSpec(memory_space=pltpu.VMEM)


def inv_rms(rows):
    return lax.rsqrt(jnp.mean(rows * rows, axis=-1, keepdims=True) + EPSILON)


def norm_back(rows, gain, grad):
    r = inv_rms(rows)
    weighted = gain * grad
    d_gain = jnp.sum(grad * rows * r, axis=0, keepdims=True)
    d_rows = r * weighted - rows * (r * r * r) * jnp.mean(weighted * rows, axis=-1, keepdims=True)
    return d_rows, d_gain


def offsets_of(mesh_sizes, axes):
    sizes = [mesh_sizes[a] for a in axes]
    return [o for o in itertools.product(*[range(s) for s in sizes]) if any(o)]


class Wire:
    def __init__(self, mesh_sizes, send_sem, recv_sem):
        self.sizes = mesh_sizes
        self.send_sem, self.recv_sem = send_sem, recv_sem
        self.used = 0

    def me(self, axes):
        return tuple(lax.axis_index(a) for a in axes)

    def peers(self, axes):
        mine = self.me(axes)
        return [
            tuple(lax.rem(m + o, self.sizes[a]) for m, o, a in zip(mine, off, axes))
            for off in offsets_of(self.sizes, axes)
        ]

    def barrier(self, axes_list):
        sem = pltpu.get_barrier_semaphore()
        count = 0
        seen = set()
        for axes in axes_list:
            for off in offsets_of(self.sizes, axes):
                key = tuple(sorted((a, o) for a, o in zip(axes, off) if o))
                if key in seen:
                    continue
                seen.add(key)
                ids = {a: lax.rem(lax.axis_index(a) + o, self.sizes[a]) for a, o in key}
                pl.semaphore_signal(sem, inc=1, device_id=ids, device_id_type=MESH)
                count += 1
        pl.semaphore_wait(sem, count)

    def send(self, axes, source, target):
        copies = []
        for k, peer in enumerate(self.peers(axes)):
            copy = pltpu.make_async_remote_copy(
                src_ref=source(peer),
                dst_ref=target(k),
                send_sem=self.send_sem.at[self.used],
                recv_sem=self.recv_sem.at[self.used],
                device_id=dict(zip(axes, peer)),
                device_id_type=MESH,
            )
            copy.start()
            copies.append(copy)
            self.used += 1
        return copies

    def gather(self, axis, source, out):
        mine = lax.axis_index(axis)
        return self.send((axis,), lambda peer: source, lambda k: out.at[mine])

    def scatter(self, axes, source, landing):
        def block(peer):
            ref = source
            for p in peer:
                ref = ref.at[p]
            return ref

        return self.send(axes, block, lambda k: landing.at[k])


def wait_recv(copies):
    for copy in copies:
        copy.wait_recv()


def wait_send(copies):
    for copy in copies:
        copy.wait_send()


def n_peers(mesh_sizes, axes):
    return len(offsets_of(mesh_sizes, axes))


class Plan:
    def __init__(self, sizes, gathers=(), sums=(), main=None):
        self.sizes = sizes
        self.gathers = list(gathers)
        self.sums = list(sums)


def call(cid, sizes, body, inputs, outs, scratch, copies):
    return pl.pallas_call(
        body,
        out_shape=outs,
        in_specs=[vmem()] * len(inputs),
        out_specs=tuple(vmem() for _ in outs),
        scratch_shapes=list(scratch)
        + [pltpu.SemaphoreType.DMA((copies,)), pltpu.SemaphoreType.DMA((copies,))],
        compiler_params=pltpu.CompilerParams(collective_id=cid, has_side_effects=True),
    )(*inputs)


GROUP = ("shard", "context")


def block_sum(source, mine, landing, count):
    own = source
    for m in mine:
        own = own.at[m]
    total = own[...].astype(F32)
    for k in range(count):
        total = total + landing[k].astype(F32)
    return total


def comm(cid, sizes, gathers, sums, reduces, epilogue, extra_in, extra_out, smalls=()):
    ng, ns_, nr, nx = len(gathers), len(sums), len(reduces), len(extra_in)
    inputs = [g for g, _ in gathers] + list(sums) + [r for r, _ in reduces] + list(extra_in)
    inputs += [s for s, _ in smalls]
    nsm = len(smalls)
    outs = [jax.ShapeDtypeStruct((sizes[a],) + g.shape, g.dtype) for g, a in gathers]
    outs += [jax.ShapeDtypeStruct(s.shape[1:], BF16) for s in sums]
    second = [ax for ax, _, _ in (epilogue.second if epilogue else ())]
    outs += [
        jax.ShapeDtypeStruct((sizes[ax],) + shape, dt)
        for ax, shape, dt in (epilogue.second if epilogue else ())
    ]
    outs += list(extra_out)
    outs += [jax.ShapeDtypeStruct(s.shape, F32) for s, _ in smalls]
    group_n = n_peers(sizes, GROUP)
    scratch = [pltpu.VMEM((group_n,) + s.shape[2:], BF16) for s in sums]
    scratch += [pltpu.VMEM((sizes[a] - 1,) + r.shape[1:], r.dtype) for r, a in reduces]
    scratch += [pltpu.VMEM((n_peers(sizes, ax),) + s.shape, F32) for s, ax in smalls]
    copies = sum(sizes[a] - 1 for _, a in gathers)
    copies += ns_ * (group_n + sizes["context"] - 1)
    copies += sum(sizes[a] - 1 for _, a in reduces) + sum(sizes[a] - 1 for a in second)
    copies += sum(n_peers(sizes, ax) for _, ax in smalls)
    axes_list = [(a,) for _, a in gathers] + [(a,) for _, a in reduces] + [(a,) for a in second]
    axes_list += ([GROUP, ("context",)] if ns_ else []) + [ax for _, ax in smalls]
    n_in, n_out = len(inputs), len(outs)

    def body(*refs):
        ins, os_ = refs[:n_in], refs[n_in : n_in + n_out]
        scr, (send_sem, recv_sem) = refs[n_in + n_out : -2], refs[-2:]
        g_in, s_in = ins[:ng], ins[ng : ng + ns_]
        r_in = ins[ng + ns_ : ng + ns_ + nr]
        x_in = ins[ng + ns_ + nr : ng + ns_ + nr + nx]
        sm_in = ins[ng + ns_ + nr + nx :]
        g_out, s_out = os_[:ng], os_[ng : ng + ns_]
        e_out = os_[ng + ns_ : ng + ns_ + len(second)]
        x_out = os_[ng + ns_ + len(second) : n_out - nsm]
        sm_out = os_[n_out - nsm :]
        s_land, r_land, sm_land = scr[:ns_], scr[ns_ : ns_ + nr], scr[ns_ + nr :]
        wire = Wire(sizes, send_sem, recv_sem)
        wire.barrier(axes_list)
        pending, recvs = [], []
        r_copies = [
            wire.scatter((a,), ref, land) for ref, land, (_, a) in zip(r_in, r_land, reduces)
        ]
        s_copies = [wire.scatter(GROUP, ref, land) for ref, land in zip(s_in, s_land)]
        for ref, out, (_, a) in zip(g_in, g_out, gathers):
            c = wire.gather(a, ref, out)
            pending += c
            recvs += c
        for ref, out, (_, a) in zip(g_in, g_out, gathers):
            out[lax.axis_index(a)] = ref[...]
        totals = []
        for ref, land, c, (_, a) in zip(r_in, r_land, r_copies, reduces):
            wait_recv(c)
            totals.append(block_sum(ref, (lax.axis_index(a),), land, sizes[a] - 1))
            pending += c
        if epilogue is not None:
            blocks = epilogue.run(totals, x_in, x_out)
            for block, out, ax in zip(blocks, e_out, second):
                mine = lax.axis_index(ax)
                out[mine] = block
                c = wire.gather(ax, out.at[mine], out)
                pending += c
                recvs += c
        mine_c = lax.axis_index("context")
        for ref, land, c, out in zip(s_in, s_land, s_copies, s_out):
            wait_recv(c)
            pending += c
            total = block_sum(ref, (lax.axis_index("shard"), mine_c), land, group_n)
            out[mine_c] = low(total)
            c2 = wire.gather("context", out.at[mine_c], out)
            pending += c2
            recvs += c2
        for i, (_, axes) in enumerate(smalls):
            source = sm_in[i]
            land = sm_land[i]
            if epilogue is not None and epilogue.small_fill is not None:
                source = epilogue.small_fill(i, sm_in, x_out, sm_out)
            c = wire.send(axes, lambda peer, src=source: src, lambda k, l=land: l.at[k])
            wait_recv(c)
            wait_send(c)
            total = source[...]
            for k in range(len(c)):
                total = total + land[k]
            sm_out[i][...] = total
        wait_recv(recvs)
        wait_send(pending)

    return call(cid, sizes, body, inputs, outs, scratch, copies)


class Epilogue:
    def __init__(self, second, run, small_fill=None):
        self.second, self.run, self.small_fill = second, run, small_fill


def self_fwd_kernel(heads, dh, q, kv, seg_q, seg_k, line, mixed, probs):
    rows, span = probs.shape[1:]
    width = heads * dh
    first = lax.axis_index("context") * rows
    t = first + lax.broadcasted_iota(jnp.int32, (rows, span), 0)
    u = lax.broadcasted_iota(jnp.int32, (rows, span), 1)
    allowed = (u <= t) & (seg_q[...] == seg_k[...])
    for h in range(heads):
        cols = slice(h * dh, (h + 1) * dh)
        bias = pltpu.roll(
            jnp.broadcast_to(line[h : h + 1, :], (rows, span)), 0, 1, stride=1, stride_axis=0
        )
        s = mm_nt(q[:, cols], kv[:, cols]) + bias
        s = jnp.where(allowed, s, MASKED)
        e = jnp.exp(s - jnp.max(s, axis=1, keepdims=True))
        p = e / jnp.sum(e, axis=1, keepdims=True)
        probs[h] = p
        mixed[:, cols] = low(mm(low(p), kv[:, width + h * dh : width + (h + 1) * dh]))


def cross_fwd_kernel(heads, dh, q, kv, seg_q, seg_k, mixed, probs):
    width = heads * dh
    allowed = seg_q[...] == seg_k[...]
    for h in range(heads):
        cols = slice(h * dh, (h + 1) * dh)
        s = jnp.where(allowed, mm_nt(q[:, cols], kv[:, cols]), MASKED)
        e = jnp.exp(s - jnp.max(s, axis=1, keepdims=True))
        p = e / jnp.sum(e, axis=1, keepdims=True)
        probs[h] = p
        mixed[:, cols] = low(mm(low(p), kv[:, width + h * dh : width + (h + 1) * dh]))


def back_kernel(heads, dh, with_bias, q, kv, probs, g, dq, dkv, *diag):
    rows, span = probs.shape[1:]
    width = heads * dh
    if with_bias:
        a = lax.broadcasted_iota(jnp.int32, (rows, rows), 0)
        b = lax.broadcasted_iota(jnp.int32, (rows, rows), 1)
        flip = jnp.where(a + b == rows - 1, 1.0, 0.0).astype(BF16)
        diag[0][...] = jnp.zeros_like(diag[0])
    for h in range(heads):
        cols = slice(h * dh, (h + 1) * dh)
        vcols = slice(width + h * dh, width + (h + 1) * dh)
        p = probs[h]
        dp = mm_nt(g[:, cols], kv[:, vcols])
        ds = low(p * (dp - jnp.sum(dp * p, axis=1, keepdims=True)))
        dq[:, cols] = low(mm(ds, kv[:, cols]))
        dkv[:, cols] = low(mm_tn(ds, q[:, cols]))
        dkv[:, vcols] = low(mm_tn(low(p), g[:, cols]))
        if with_bias:
            skew = pltpu.roll(mm(flip, ds), 0, 1, stride=1, stride_axis=0)
            diag[0][h : h + 1, :] = jnp.sum(skew, axis=0, keepdims=True)


def local_call(kernel, inputs, outs):
    return pl.pallas_call(
        kernel,
        out_shape=outs,
        in_specs=[vmem()] * len(inputs),
        out_specs=tuple(vmem() for _ in outs),
    )(*inputs)


def sds(shape, dtype):
    return jax.ShapeDtypeStruct(shape, dtype)


def body(
    sizes,
    hidden,
    enc_states,
    cotangent,
    segments,
    positions,
    enc_segments,
    doc_source,
    bucket_of,
    norm_self,
    norm_cross,
    norm_ffn,
    bias_table,
    w_q,
    w_k,
    w_v,
    w_o,
    c_q,
    c_k,
    c_v,
    c_o,
    w_gate,
    w_up,
    w_down,
):
    ns, nc, nt = sizes["shard"], sizes["context"], sizes["tensor"]
    seq_count, rows, width = hidden.shape
    assert seq_count == 1
    enc_len = enc_states.shape[1]
    heads = bias_table.shape[1]
    unit = w_q.shape[1]
    dh = unit // heads
    ffn = w_gate.shape[1]
    span = nc * rows
    enc_span = nc * enc_len
    ctx = lax.axis_index("context")
    part = rows // nt
    comm_ = functools.partial(comm, sizes=sizes)

    x = hidden[0]
    cot = cotangent[0]
    enc = enc_states[0]
    gain_s, gain_c, gain_f = norm_self[None, :], norm_cross[None, :], norm_ffn[None, :]

    pack_a = jnp.concatenate([w_q, w_k, w_v, c_k], axis=1)
    pack_b = jnp.concatenate([c_v, c_q], axis=1)
    segs = jnp.concatenate([segments, enc_segments], axis=1)
    a_all, b_all, seg_all = comm_(
        0,
        gathers=[(pack_a, "shard"), (pack_b, "shard"), (segs, "context")],
        sums=[], reduces=[], epilogue=None, extra_in=[], extra_out=[],
    )
    a_all = a_all.reshape(width, 4 * unit)
    b_all = b_all.reshape(width, 2 * unit)
    wq, wk, wv, ck = (a_all[:, i * unit : (i + 1) * unit] for i in range(4))
    cv, cq = b_all[:, :unit], b_all[:, unit:]
    seg_k = seg_all[:, 0, :rows].reshape(1, span)
    enc_seg_k = seg_all[:, 0, rows:].reshape(1, enc_span)
    seg_q = segments.reshape(rows, 1)
    target = jnp.zeros_like(segments)
    for doc in range(doc_source.shape[1]):
        target = jnp.where(segments == doc, doc_source[:, doc : doc + 1], target)
    target = target.reshape(rows, 1)

    normed_self = low(x * inv_rms(x) * gain_s)
    qkv = low(mm(normed_self, a_all[:, : 3 * unit]))
    q = qkv[:, :unit]
    ekv_own = jnp.concatenate([low(mm(enc, ck)), low(mm(enc, cv))], axis=1)
    kv_all, ekv_all, wo_all, co_all = comm_(
        1,
        gathers=[(qkv[:, unit:], "context"), (ekv_own, "context"), (w_o, "shard"), (c_o, "shard")],
        sums=[], reduces=[], epilogue=None, extra_in=[], extra_out=[],
    )
    kv = kv_all.reshape(span, 2 * unit)
    ekv = ekv_all.reshape(enc_span, 2 * unit)
    wo = jnp.moveaxis(wo_all, 0, 1).reshape(unit, width)
    co = jnp.moveaxis(co_all, 0, 1).reshape(unit, width)

    flipped = bucket_of[::-1]
    twice = jnp.concatenate([flipped, flipped])
    bucket = lax.dynamic_slice(twice, (span - ctx * rows - 1,), (span,))
    onehot = (bucket[None, :] == jnp.arange(bias_table.shape[0], dtype=jnp.int32)[:, None]).astype(F32)
    line = lax.dot_general(
        bias_table, onehot, (((0,), (0,)), ((), ())), precision=lax.Precision.HIGHEST
    )
    mixed, probs = local_call(
        functools.partial(self_fwd_kernel, heads, dh),
        [q, kv, seg_q, seg_k, line],
        [sds((rows, unit), BF16), sds((heads, rows, span), F32)],
    )

    def fwd_step(totals, x_in, x_out):
        rows_in, gain = x_in
        base = rows_in[lax.axis_index("tensor")] if len(rows_in.shape) == 3 else rows_in[...]
        after = base + totals[0]
        x_out[0][...] = after
        return [low(after * inv_rms(after) * gain[...])]

    shape3 = (part, width)
    ep_fwd = Epilogue([("tensor", shape3, BF16)], fwd_step)
    part_self = low(mm(mixed, wo)).reshape(nt, part, width)
    gate_all, up_all, normed_cross, after_self = comm_(
        2,
        gathers=[(w_gate, "shard"), (w_up, "shard")],
        sums=[], reduces=[(part_self, "tensor")], epilogue=ep_fwd,
        extra_in=[x.reshape(nt, part, width), gain_c], extra_out=[sds(shape3, F32)],
    )
    wg, wu = gate_all.reshape(width, ffn), up_all.reshape(width, ffn)
    normed_cross = normed_cross.reshape(rows, width)

    cqs = low(mm(normed_cross, cq))
    cmixed, cprobs = local_call(
        functools.partial(cross_fwd_kernel, heads, dh),
        [cqs, ekv, target, enc_seg_k],
        [sds((rows, unit), BF16), sds((heads, rows, enc_span), F32)],
    )
    part_cross = low(mm(cmixed, co)).reshape(nt, part, width)
    down_all, normed_ffn, after_cross = comm_(
        3,
        gathers=[(w_down, "shard")],
        sums=[], reduces=[(part_cross, "tensor")], epilogue=ep_fwd,
        extra_in=[after_self, gain_f], extra_out=[sds(shape3, F32)],
    )
    wd = jnp.moveaxis(down_all, 0, 1).reshape(ffn, width)
    normed_ffn = normed_ffn.reshape(rows, width)

    gate_pre, up_pre = mm(normed_ffn, wg), mm(normed_ffn, wu)
    top_low = low(cot)
    d_units = mm_nt(top_low, wd)
    k0, k1 = 0.7978845608028654, 0.044715
    sq = gate_pre * gate_pre
    th = jnp.tanh(k0 * (gate_pre + k1 * gate_pre * sq))
    gelu = 0.5 * gate_pre * (1.0 + th)
    d_gelu = 0.5 * (1.0 + th) + 0.5 * gate_pre * (1.0 - th * th) * k0 * (1.0 + 3.0 * k1 * sq)
    units = low(gelu * up_pre)
    d_gate = low(d_units * up_pre * d_gelu)
    d_up = low(d_units * gelu)
    part_out = low(mm(units, wd)).reshape(nt, part, width)
    part_ffn = low(mm_nt(d_gate, wg) + mm_nt(d_up, wu)).reshape(nt, part, width)

    def wide(grad):
        return low(grad).reshape(ns, nc, width // (ns * nc), grad.shape[1])

    def tall(grad):
        r, c = grad.shape
        return jnp.moveaxis(low(grad).reshape(nc, r // nc, ns, c // ns), 2, 0)

    g_down = tall(mm_tn(units, top_low))
    g_gate = wide(mm_tn(normed_ffn, d_gate))
    g_up = wide(mm_tn(normed_ffn, d_up))

    def back_step(totals, x_in, x_out):
        rows_in, gain, above = x_in
        over = above[lax.axis_index("tensor")] if len(above.shape) == 3 else above[...]
        d_rows, d_gain = norm_back(rows_in[...], gain[...], totals[0])
        grad = over + d_rows
        x_out[0][...] = grad
        x_out[1][...] = d_gain
        return [low(grad)]

    ep_back = Epilogue([("tensor", shape3, BF16)], back_step)
    back_out = [sds(shape3, F32), sds((1, width), F32)]
    down_sum, cross_low_grad, cross_grad, dg_ffn = comm_(
        4,
        gathers=[], sums=[g_down], reduces=[(part_ffn, "tensor")], epilogue=ep_back,
        extra_in=[after_cross, gain_f, cot.reshape(nt, part, width)], extra_out=back_out,
    )
    cross_low_grad = cross_low_grad.reshape(rows, width)
    d_cmixed = low(mm_nt(cross_low_grad, co))
    d_cq, d_ekv = local_call(
        functools.partial(back_kernel, heads, dh, False),
        [cqs, ekv, cprobs, d_cmixed],
        [sds((rows, unit), BF16), sds((enc_span, 2 * unit), BF16)],
    )
    part_ncross = low(mm_nt(d_cq, cq)).reshape(nt, part, width)

    def cross_back_step(totals, x_in, x_out):
        x_out[2][...] = low(totals[1])
        return back_step(totals, x_in, x_out)

    gate_sum, up_sum, self_low_grad, self_grad, dg_cross, d_ekv_own = comm_(
        5,
        gathers=[], sums=[g_gate, g_up],
        reduces=[
            (part_ncross, "tensor"),
            (d_ekv.reshape(nc, enc_len, 2 * unit), "context"),
        ],
        epilogue=Epilogue([("tensor", shape3, BF16)], cross_back_step),
        extra_in=[after_self, gain_c, cross_grad],
        extra_out=back_out + [sds((enc_len, 2 * unit), BF16)],
    )
    self_low_grad = self_low_grad.reshape(rows, width)
    d_mixed = low(mm_nt(self_low_grad, wo))
    d_q, d_kv, diag = local_call(
        functools.partial(back_kernel, heads, dh, True),
        [q, kv, probs, d_mixed],
        [sds((rows, unit), BF16), sds((span, 2 * unit), BF16), sds((8, span), F32)],
    )

    g_co = tall(mm_tn(cmixed, cross_low_grad))
    g_wo = tall(mm_tn(mixed, self_low_grad))
    g_cq = mm_tn(normed_cross, d_cq)
    g_ckv = mm_tn(enc, d_ekv_own)
    g_cross = wide(jnp.concatenate([g_cq, g_ckv], axis=1))
    d_ek, d_ev = d_ekv_own[:, :unit], d_ekv_own[:, unit:]
    part_enc = low(mm_nt(d_ek, ck) + mm_nt(d_ev, cv)).reshape(nt, enc_len // nt, width)

    def mid_step(totals, x_in, x_out):
        base = x_in[0][...] - x_in[1][lax.axis_index("tensor")]
        x_out[0][...] = low(totals[0])
        return [low(totals[1] + base), low(totals[2])]

    co_sum, wo_sum, cross_sum, out_delta, d_enc, d_kv_own = comm_(
        6,
        gathers=[], sums=[g_co, g_wo, g_cross],
        reduces=[
            (d_kv.reshape(nc, rows, 2 * unit), "context"),
            (part_out, "tensor"),
            (part_enc, "tensor"),
        ],
        epilogue=Epilogue(
            [("tensor", shape3, BF16), ("tensor", (enc_len // nt, width), BF16)], mid_step
        ),
        extra_in=[after_cross, x.reshape(nt, part, width)],
        extra_out=[sds((rows, 2 * unit), BF16)],
    )
    d_qkv = jnp.concatenate([d_q, d_kv_own], axis=1)
    part_nself = low(mm_nt(d_qkv, a_all[:, : 3 * unit])).reshape(nt, part, width)
    g_self = wide(mm_tn(normed_self, d_qkv))

    lane = jnp.arange(span, dtype=jnp.int32)
    dist = lax.rem(ctx * rows + (rows - 1) - lane + span, span)
    del dist
    bucket_d = lax.dynamic_slice(twice, (lax.rem(2 * span - ctx * rows - rows, span),), (span,))
    onehot_d = (bucket_d[None, :] == jnp.arange(bias_table.shape[0], dtype=jnp.int32)[:, None]).astype(F32)
    g_bias = lax.dot_general(
        diag, onehot_d, (((1,), (1,)), ((), ())), precision=lax.Precision.HIGHEST
    )

    def last_step(totals, x_in, x_out):
        rows_in, gain, above, cot_in, dgf, dgc = x_in
        d_rows, d_gain = norm_back(rows_in[lax.axis_index("tensor")], gain[...], totals[0])
        x_out[0][0:1, :] = dgf[...]
        x_out[0][1:2, :] = dgc[...]
        x_out[0][2:3, :] = d_gain
        x_out[0][3:8, :] = jnp.zeros_like(x_out[0][3:8, :])
        return [low(above[...] - cot_in[lax.axis_index("tensor")] + d_rows)]

    def small_fill(i, sm_in, x_out, sm_out):
        return [sm_in[0], x_out[0], sm_out[1]][i]

    gains0 = jnp.zeros((8, width), F32)
    self_sum, hid_delta, _, bias_sum, _, gain_sum = comm_(
        7,
        gathers=[], sums=[g_self], reduces=[(part_nself, "tensor")],
        epilogue=Epilogue([("tensor", shape3, BF16)], last_step, small_fill),
        extra_in=[
            x.reshape(nt, part, width), gain_s, self_grad, cot.reshape(nt, part, width),
            dg_ffn, dg_cross,
        ],
        extra_out=[sds((8, width), F32)],
        smalls=[(g_bias, GROUP), (gains0, ("tensor",)), (gains0, GROUP)],
    )

    def wide_out(total):
        return total.reshape(width // ns, total.shape[-1]).astype(F32)

    def tall_out(total):
        return total.reshape(total.shape[0] * total.shape[1], total.shape[2]).astype(F32)

    self_w, cross_w = wide_out(self_sum), wide_out(cross_sum)
    return (
        (x + out_delta.reshape(rows, width).astype(F32))[None],
        (cot + hid_delta.reshape(rows, width).astype(F32))[None],
        d_enc.reshape(1, enc_len, width).astype(F32),
        gain_sum[2],
        gain_sum[1],
        gain_sum[0],
        bias_sum[:heads].T,
        self_w[:, :unit],
        self_w[:, unit : 2 * unit],
        self_w[:, 2 * unit :],
        tall_out(wo_sum),
        cross_w[:, :unit],
        cross_w[:, unit : 2 * unit],
        cross_w[:, 2 * unit :],
        tall_out(co_sum),
        wide_out(gate_sum),
        wide_out(up_sum),
        tall_out(down_sum),
    )


def solution(mesh):
    tok = P("shard", "context", None)
    ids = P("shard", "context")
    wide, tall = P("shard", "tensor"), P("tensor", "shard")
    in_specs = (tok, tok, tok, ids, ids, ids, P("shard", None), P(), P(), P(), P(), P(None, "tensor"))
    in_specs += (wide, wide, wide, tall) * 2 + (wide, wide, tall)
    out_specs = (tok, tok, tok, P(), P(), P(), P(None, "tensor"))
    out_specs += (wide, wide, wide, tall) * 2 + (wide, wide, tall)
    sizes = {a: mesh.shape[a] for a in ("shard", "context", "tensor")}
    return jax.shard_map(
        functools.partial(body, sizes),
        mesh=mesh,
        in_specs=in_specs,
        out_specs=out_specs,
        check_vma=False,
    )
```

```python
import functools
import itertools

import jax
import jax.numpy as jnp
from jax import lax
from jax.experimental import pallas as pl
from jax.experimental.pallas import tpu as pltpu
from jax.sharding import PartitionSpec as P

EPSILON = 1e-06
MASKED = -1e30
MESH = pl.DeviceIdType.MESH
BF16 = jnp.bfloat16
F32 = jnp.float32


def low(values):
    return values.astype(BF16)


def mm(left, right):
    return jnp.dot(left, right, preferred_element_type=F32)


def mm_tn(left, right):
    return lax.dot_general(
        left, right, (((0,), (0,)), ((), ())), preferred_element_type=F32
    )


def mm_nt(left, right):
    return lax.dot_general(
        left, right, (((1,), (1,)), ((), ())), preferred_element_type=F32
    )


def vmem():
    return pl.BlockSpec(memory_space=pltpu.VMEM)


def inv_rms(rows):
    return lax.rsqrt(jnp.mean(rows * rows, axis=-1, keepdims=True) + EPSILON)


def norm_back(rows, gain, grad):
    r = inv_rms(rows)
    weighted = gain * grad
    d_gain = jnp.sum(grad * rows * r, axis=0, keepdims=True)
    d_rows = r * weighted - rows * (r * r * r) * jnp.mean(weighted * rows, axis=-1, keepdims=True)
    return d_rows, d_gain


class Wire:
    def __init__(self, sizes, send_sem, recv_sem):
        self.sizes = sizes
        self.send_sem, self.recv_sem = send_sem, recv_sem
        self.used = 0

    def peers(self, kind):
        ns, nc = self.sizes["shard"], self.sizes["context"]
        if isinstance(kind, tuple):
            a, n = kind[1], self.sizes[kind[1]]
            me = lax.axis_index(a)
            return [{a: lax.rem(me + o, n)} for o in range(1, n)]
        ms, mc = lax.axis_index("shard"), lax.axis_index("context")
        hi, lo = mc // 2, lax.rem(mc, 2)
        if kind == "sibling":
            return [{"context": 2 * hi + 1 - lo}]
        if kind == "hi":
            return [{"context": 2 * lax.rem(hi + o, nc // 2) + lo} for o in range(1, nc // 2)]
        if kind == "apart":
            offs = [o for o in itertools.product(range(ns), range(nc // 2)) if any(o)]
            return [
                {"shard": lax.rem(ms + o, ns), "context": 2 * lax.rem(hi + p, nc // 2) + lo}
                for o, p in offs
            ]
        offs = [o for o in itertools.product(range(ns), range(nc)) if any(o)]
        return [{"shard": lax.rem(ms + o, ns), "context": lax.rem(mc + p, nc)} for o, p in offs]

    def barrier(self, kinds):
        sem = pltpu.get_barrier_semaphore()
        count = 0
        for kind in dict.fromkeys(kinds):
            for peer in self.peers(kind):
                pl.semaphore_signal(sem, inc=1, device_id=peer, device_id_type=MESH)
                count += 1
        pl.semaphore_wait(sem, count)

    def send(self, kind, source, target):
        copies = []
        for k, peer in enumerate(self.peers(kind)):
            copies.append(self.one(peer, source(peer), target(k)))
        return copies

    def one(self, peer, source, target):
        copy = pltpu.make_async_remote_copy(
            src_ref=source,
            dst_ref=target,
            send_sem=self.send_sem.at[self.used],
            recv_sem=self.recv_sem.at[self.used],
            device_id=peer,
            device_id_type=MESH,
        )
        copy.start()
        self.used += 1
        return copy


def wait_recv(copies):
    for copy in copies:
        copy.wait_recv()


def wait_send(copies):
    for copy in copies:
        copy.wait_send()


def n_peers(sizes, kind):
    if isinstance(kind, tuple):
        return sizes[kind[1]] - 1
    ns, nc = sizes["shard"], sizes["context"]
    return {"sibling": 1, "hi": nc // 2 - 1, "apart": ns * nc // 2 - 1, "group": ns * nc - 1}[kind]


def call(cid, sizes, body, inputs, outs, scratch, copies):
    return pl.pallas_call(
        body,
        out_shape=outs,
        in_specs=[vmem()] * len(inputs),
        out_specs=tuple(vmem() for _ in outs),
        scratch_shapes=list(scratch)
        + [pltpu.SemaphoreType.DMA((copies,)), pltpu.SemaphoreType.DMA((copies,))],
        compiler_params=pltpu.CompilerParams(collective_id=cid, has_side_effects=True),
    )(*inputs)


def comm(cid, sizes, gathers, sums, reduces, epilogue, extra_in, extra_out, smalls=()):
    ns, nc = sizes["shard"], sizes["context"]
    nh = nc // 2
    ng, nsum, nr, nx, nsm = len(gathers), len(sums), len(reduces), len(extra_in), len(smalls)
    inputs = [g for g, _ in gathers] + list(sums) + [r for r, _ in reduces] + list(extra_in)
    inputs += [s for s, _ in smalls]
    outs, copies, kinds = [], 0, []
    for g, how in gathers:
        if how == "shard":
            outs.append(jax.ShapeDtypeStruct((ns,) + g.shape, g.dtype))
            copies += 2 * (ns - 1)
            kinds += [("axis", "shard"), "sibling"]
        elif how == "context":
            outs.append(jax.ShapeDtypeStruct((nh, 2) + g.shape, g.dtype))
            copies += 1 + 2 * (nh - 1)
            kinds += ["hi", "sibling"]
        else:
            axis = how.split(":")[1]
            outs.append(jax.ShapeDtypeStruct((sizes[axis],) + g.shape, g.dtype))
            copies += sizes[axis] - 1
            kinds.append(("axis", axis))
    outs += [jax.ShapeDtypeStruct(s.shape[1:], BF16) for s in sums]
    apart = n_peers(sizes, "apart")
    copies += nsum * (1 + apart + 1 + 2 * (nh - 1))
    kinds += ["sibling", "apart", "hi"] if nsum else []
    second = epilogue.second if epilogue else []
    outs += [jax.ShapeDtypeStruct((sizes[ax],) + shape, dt) for ax, shape, dt in second]
    axes = [a for _, a in reduces] + [ax for ax, _, _ in second]
    copies += sum(sizes[a] - 1 for a in axes)
    kinds += [("axis", a) for a in axes]
    outs += list(extra_out)
    outs += [jax.ShapeDtypeStruct(s.shape, F32) for s, _ in smalls]
    copies += sum(n_peers(sizes, kind) for _, kind in smalls)
    kinds += [kind for _, kind in smalls]
    scratch = []
    for s in sums:
        scratch += [
            pltpu.VMEM((ns,) + s.shape[2:], BF16),
            pltpu.VMEM((ns,) + s.shape[2:], BF16),
            pltpu.VMEM((apart,) + s.shape[3:], BF16),
        ]
    scratch += [pltpu.VMEM((sizes[a] - 1,) + r.shape[1:], r.dtype) for r, a in reduces]
    scratch += [pltpu.VMEM((n_peers(sizes, kind),) + s.shape, F32) for s, kind in smalls]
    n_in, n_out = len(inputs), len(outs)

    def body(*refs):
        ins, os_ = refs[:n_in], refs[n_in : n_in + n_out]
        scr, (send_sem, recv_sem) = refs[n_in + n_out : -2], refs[-2:]
        g_in, s_in = ins[:ng], ins[ng : ng + nsum]
        r_in = ins[ng + nsum : ng + nsum + nr]
        x_in = ins[ng + nsum + nr : ng + nsum + nr + nx]
        sm_in = ins[ng + nsum + nr + nx :]
        g_out, s_out = os_[:ng], os_[ng : ng + nsum]
        e_out = os_[ng + nsum : ng + nsum + len(second)]
        x_out = os_[ng + nsum + len(second) : n_out - nsm]
        sm_out = os_[n_out - nsm :]
        s_scr = [scr[3 * i : 3 * i + 3] for i in range(nsum)]
        r_land, sm_land = scr[3 * nsum : 3 * nsum + nr], scr[3 * nsum + nr :]
        ms, mc = lax.axis_index("shard"), lax.axis_index("context")
        hi, lo = mc // 2, lax.rem(mc, 2)
        sibling = {"context": 2 * hi + 1 - lo}
        wire = Wire(sizes, send_sem, recv_sem)
        wire.barrier(kinds)
        pending, recvs, forwards = [], [], []

        r_copies = [
            wire.send(
                ("axis", a), lambda p, ref=ref, a=a: ref.at[p[a]], lambda k, land=land: land.at[k]
            )
            for ref, land, (_, a) in zip(r_in, r_land, reduces)
        ]
        s_first = [wire.one(sibling, ref.at[:, 1 - lo], l[0]) for ref, l in zip(s_in, s_scr)]
        for ref, out, (_, how) in zip(g_in, g_out, gathers):
            if how == "shard":
                c = wire.send(
                    ("axis", "shard"),
                    lambda p, ref=ref: ref.at[lo],
                    lambda k, out=out: out.at[ms, lo],
                )
                slots = [out.at[lax.rem(ms + ns - o, ns), lo] for o in range(1, ns)]
                forwards += list(zip(c, slots))
            elif how == "context":
                c = wire.send(
                    "hi", lambda p, ref=ref: ref, lambda k, out=out: out.at[hi, lo]
                )
                slots = [out.at[lax.rem(hi + nh - o, nh), lo] for o in range(1, nh)]
                forwards += list(zip(c, slots))
                own = wire.one(sibling, ref, out.at[hi, lo])
                recvs.append(own)
                pending.append(own)
            else:
                axis = how.split(":")[1]
                me = lax.axis_index(axis)
                c = wire.send(
                    ("axis", axis),
                    lambda p, ref=ref: ref,
                    lambda k, out=out, me=me: out.at[me],
                )
                recvs += c
            pending += c
        for ref, out, (_, how) in zip(g_in, g_out, gathers):
            if how == "shard":
                out[ms] = ref[...]
            elif how == "context":
                out[hi, lo] = ref[...]
            else:
                out[lax.axis_index(how.split(":")[1])] = ref[...]

        s_second = []
        for ref, c, (land, pair, others) in zip(s_in, s_first, s_scr):
            c.wait_recv()
            for i in range(ns):
                pair[i] = low(ref[i, lo].astype(F32) + land[i].astype(F32))
            s_second.append(
                wire.send(
                    "apart",
                    lambda p, pair=pair: pair.at[p["shard"], p["context"] // 2],
                    lambda k, others=others: others.at[k],
                )
            )
            pending.append(c)

        totals = []
        for ref, land, c, (_, a) in zip(r_in, r_land, r_copies, reduces):
            wait_recv(c)
            total = ref[lax.axis_index(a)].astype(F32)
            for k in range(sizes[a] - 1):
                total = total + land[k].astype(F32)
            totals.append(total)
            pending += c
        if epilogue is not None:
            blocks = epilogue.run(totals, x_in, x_out)
            for block, out, (ax, _, _) in zip(blocks, e_out, second):
                mine = lax.axis_index(ax)
                out[mine] = block
                c = wire.send(
                    ("axis", ax),
                    lambda p, out=out, mine=mine: out.at[mine],
                    lambda k, out=out, mine=mine: out.at[mine],
                )
                pending += c
                recvs += c

        for c, slot in forwards:
            c.wait_recv()
            f = wire.one(sibling, slot, slot)
            pending.append(f)
            recvs.append(f)
        forwards = []
        for c, (land, pair, others), out in zip(s_second, s_scr, s_out):
            wait_recv(c)
            pending += c
            total = pair[ms, hi].astype(F32)
            for k in range(apart):
                total = total + others[k].astype(F32)
            out[lo, hi] = low(total)
            c2 = wire.send(
                "hi", lambda p, out=out: out.at[lo, hi], lambda k, out=out: out.at[lo, hi]
            )
            pending += c2
            forwards += [
                (c3, out.at[lo, lax.rem(hi + nh - o, nh)]) for c3, o in zip(c2, range(1, nh))
            ]
            own = wire.one(sibling, out.at[lo, hi], out.at[lo, hi])
            pending.append(own)
            recvs.append(own)
        for i, (_, kind) in enumerate(smalls):
            source = epilogue.small_fill(i, sm_in, x_out, sm_out)
            land = sm_land[i]
            c = wire.send(kind, lambda p, src=source: src, lambda k, l=land: l.at[k])
            wait_recv(c)
            wait_send(c)
            total = source[...]
            for k in range(len(c)):
                total = total + land[k]
            sm_out[i][...] = total
        for c, slot in forwards:
            c.wait_recv()
            f = wire.one(sibling, slot, slot)
            pending.append(f)
            recvs.append(f)
        wait_recv(recvs)
        wait_send(pending)

    return call(cid, sizes, body, inputs, outs, scratch, copies)


class Epilogue:
    def __init__(self, second, run, small_fill=None):
        self.second, self.run, self.small_fill = second, run, small_fill


def one_hot(ids, values):
    row = lax.broadcasted_iota(jnp.int32, (8, ids.shape[1]), 0)
    wanted = row
    if values is not None:
        wanted = jnp.full_like(row, -1)
        for r, value in enumerate(values):
            wanted = jnp.where(row == r, value, wanted)
    return jnp.where(wanted == ids, 1.0, 0.0).astype(F32)


def same_doc(left, right):
    return mm_tn(left, right) > 0.5


def self_fwd_kernel(heads, dh, q, kv, seg_q, seg_k, line, mixed, probs):
    rows, span = probs.shape[1:]
    width = heads * dh
    first = lax.axis_index("context") * rows
    t = first + lax.broadcasted_iota(jnp.int32, (rows, span), 0)
    u = lax.broadcasted_iota(jnp.int32, (rows, span), 1)
    allowed = (u <= t) & same_doc(one_hot(seg_q[...], None), one_hot(seg_k[...], None))
    for h in range(heads):
        cols = slice(h * dh, (h + 1) * dh)
        bias = pltpu.roll(
            jnp.broadcast_to(line[h : h + 1, :], (rows, span)), 0, 1, stride=1, stride_axis=0
        )
        s = mm_nt(q[:, cols], kv[:, cols]) + bias
        s = jnp.where(allowed, s, MASKED)
        e = jnp.exp(s - jnp.max(s, axis=1, keepdims=True))
        p = e / jnp.sum(e, axis=1, keepdims=True)
        probs[h] = p
        mixed[:, cols] = low(mm(low(p), kv[:, width + h * dh : width + (h + 1) * dh]))


def cross_fwd_kernel(heads, dh, q, kv, seg_q, seg_k, source, mixed, probs):
    width = heads * dh
    docs = [source[0, d] for d in range(source.shape[1])]
    allowed = same_doc(one_hot(seg_q[...], None), one_hot(seg_k[...], docs))
    for h in range(heads):
        cols = slice(h * dh, (h + 1) * dh)
        s = jnp.where(allowed, mm_nt(q[:, cols], kv[:, cols]), MASKED)
        e = jnp.exp(s - jnp.max(s, axis=1, keepdims=True))
        p = e / jnp.sum(e, axis=1, keepdims=True)
        probs[h] = p
        mixed[:, cols] = low(mm(low(p), kv[:, width + h * dh : width + (h + 1) * dh]))


def back_kernel(heads, dh, with_bias, q, kv, probs, g, dq, dkv, *diag):
    rows, span = probs.shape[1:]
    width = heads * dh
    if with_bias:
        a = lax.broadcasted_iota(jnp.int32, (rows, rows), 0)
        b = lax.broadcasted_iota(jnp.int32, (rows, rows), 1)
        flip = jnp.where(a + b == rows - 1, 1.0, 0.0).astype(BF16)
        diag[0][...] = jnp.zeros_like(diag[0])
    for h in range(heads):
        cols = slice(h * dh, (h + 1) * dh)
        vcols = slice(width + h * dh, width + (h + 1) * dh)
        p = probs[h]
        dp = mm_nt(g[:, cols], kv[:, vcols])
        ds = low(p * (dp - jnp.sum(dp * p, axis=1, keepdims=True)))
        dq[:, cols] = low(mm(ds, kv[:, cols]))
        dkv[:, cols] = low(mm_tn(ds, q[:, cols]))
        dkv[:, vcols] = low(mm_tn(low(p), g[:, cols]))
        if with_bias:
            skew = pltpu.roll(mm(flip, ds), 0, 1, stride=1, stride_axis=0)
            diag[0][h : h + 1, :] = jnp.sum(skew, axis=0, keepdims=True)


def local_call(kernel, inputs, outs, scalars=0):
    return pl.pallas_call(
        kernel,
        out_shape=outs,
        in_specs=[vmem()] * (len(inputs) - scalars)
        + [pl.BlockSpec(memory_space=pltpu.SMEM)] * scalars,
        out_specs=tuple(vmem() for _ in outs),
    )(*inputs)


def sds(shape, dtype):
    return jax.ShapeDtypeStruct(shape, dtype)


def body(
    sizes,
    hidden,
    enc_states,
    cotangent,
    segments,
    positions,
    enc_segments,
    doc_source,
    bucket_of,
    norm_self,
    norm_cross,
    norm_ffn,
    bias_table,
    w_q,
    w_k,
    w_v,
    w_o,
    c_q,
    c_k,
    c_v,
    c_o,
    w_gate,
    w_up,
    w_down,
):
    ns, nc, nt = sizes["shard"], sizes["context"], sizes["tensor"]
    seq_count, rows, width = hidden.shape
    assert seq_count == 1
    enc_len = enc_states.shape[1]
    heads = bias_table.shape[1]
    unit = w_q.shape[1]
    dh = unit // heads
    ffn = w_gate.shape[1]
    span = nc * rows
    enc_span = nc * enc_len
    ctx = lax.axis_index("context")
    part = rows // nt
    comm_ = functools.partial(comm, sizes=sizes)

    x = hidden[0]
    cot = cotangent[0]
    enc = enc_states[0]
    gain_s, gain_c, gain_f = norm_self[None, :], norm_cross[None, :], norm_ffn[None, :]

    def halves(array):
        return array.reshape(2, array.shape[0] // 2, array.shape[1])

    def columns(gathered):
        n, _, r, c = gathered.shape
        return jnp.moveaxis(gathered.reshape(n, 2 * r, c), 0, 1).reshape(2 * r, n * c)

    segs = jnp.concatenate([segments, enc_segments], axis=1)
    pack = jnp.concatenate([w_q.T, w_k.T, w_v.T], axis=0)
    qkv_all, seg_all = comm_(
        0,
        gathers=[(halves(pack), "shard"), (segs, "axis:context")],
        sums=[], reduces=[], epilogue=None, extra_in=[], extra_out=[],
    )
    w_qkv = columns(qkv_all)
    seg_k = seg_all[:, 0, :rows].reshape(1, span)
    enc_seg_k = seg_all[:, 0, rows:].reshape(1, enc_span)

    normed_self = low(x * inv_rms(x) * gain_s)
    qkv = low(mm_nt(normed_self, w_qkv))
    q = qkv[:, :unit]
    pack = jnp.concatenate([c_k.T, c_v.T, w_o], axis=0)
    kv_all, mid_all = comm_(
        1,
        gathers=[(qkv[:, unit:], "context"), (halves(pack), "shard")],
        sums=[], reduces=[], epilogue=None, extra_in=[], extra_out=[],
    )
    kv = kv_all.reshape(span, 2 * unit)
    mid_w = columns(mid_all)
    ckv, wo = mid_w[: 2 * unit], mid_w[2 * unit :]
    ekv_own = low(mm_nt(enc, ckv))

    flipped = bucket_of[::-1]
    twice = jnp.concatenate([flipped, flipped])
    bucket = lax.dynamic_slice(twice, (span - ctx * rows - 1,), (span,))
    onehot = (bucket[None, :] == jnp.arange(bias_table.shape[0], dtype=jnp.int32)[:, None]).astype(F32)
    line = lax.dot_general(
        bias_table, onehot, (((0,), (0,)), ((), ())), precision=lax.Precision.HIGHEST
    )
    mixed, probs = local_call(
        functools.partial(self_fwd_kernel, heads, dh),
        [q, kv, segments, seg_k, line],
        [sds((rows, unit), BF16), sds((heads, rows, span), F32)],
    )

    def fwd_step(totals, x_in, x_out):
        rows_in, gain = x_in
        base = rows_in[lax.axis_index("tensor")] if len(rows_in.shape) == 3 else rows_in[...]
        after = base + totals[0]
        x_out[0][...] = after
        return [low(after * inv_rms(after) * gain[...])]

    shape3 = (part, width)
    ep_fwd = Epilogue([("tensor", shape3, BF16)], fwd_step)
    part_self = low(mm(mixed, wo)).reshape(nt, part, width)
    pack = jnp.concatenate([c_q.T, c_o], axis=0)
    ekv_all, cqo_all, gate_all, up_all, normed_cross, after_self = comm_(
        2,
        gathers=[
            (ekv_own, "context"),
            (halves(pack), "shard"),
            (halves(w_gate), "shard"),
            (halves(w_up), "shard"),
        ],
        sums=[], reduces=[(part_self, "tensor")], epilogue=ep_fwd,
        extra_in=[x.reshape(nt, part, width), gain_c], extra_out=[sds(shape3, F32)],
    )
    ekv = ekv_all.reshape(enc_span, 2 * unit)
    cqo = columns(cqo_all)
    cq, co = cqo[:unit], cqo[unit:]
    wg, wu = gate_all.reshape(width, ffn), up_all.reshape(width, ffn)
    normed_cross = normed_cross.reshape(rows, width)

    cqs = low(mm_nt(normed_cross, cq))
    cmixed, cprobs = local_call(
        functools.partial(cross_fwd_kernel, heads, dh),
        [cqs, ekv, segments, enc_seg_k, doc_source],
        [sds((rows, unit), BF16), sds((heads, rows, enc_span), F32)],
        scalars=1,
    )
    part_cross = low(mm(cmixed, co)).reshape(nt, part, width)
    down_all, normed_ffn, after_cross = comm_(
        3,
        gathers=[(halves(w_down), "shard")],
        sums=[], reduces=[(part_cross, "tensor")], epilogue=ep_fwd,
        extra_in=[after_self, gain_f], extra_out=[sds(shape3, F32)],
    )
    wd = columns(down_all)
    normed_ffn = normed_ffn.reshape(rows, width)

    gate_pre, up_pre = mm(normed_ffn, wg), mm(normed_ffn, wu)
    top_low = low(cot)
    d_units = mm_nt(top_low, wd)
    k0, k1 = 0.7978845608028654, 0.044715
    sq = gate_pre * gate_pre
    th = jnp.tanh(k0 * (gate_pre + k1 * gate_pre * sq))
    gelu = 0.5 * gate_pre * (1.0 + th)
    d_gelu = 0.5 * (1.0 + th) + 0.5 * gate_pre * (1.0 - th * th) * k0 * (1.0 + 3.0 * k1 * sq)
    units = low(gelu * up_pre)
    d_gate = low(d_units * up_pre * d_gelu)
    d_up = low(d_units * gelu)
    part_out = low(mm(units, wd)).reshape(nt, part, width)
    part_ffn = low(mm_nt(d_gate, wg) + mm_nt(d_up, wu)).reshape(nt, part, width)

    def wide(grad):
        return low(grad).reshape(ns, 2, nc // 2, width // (ns * nc), grad.shape[1])

    def tall(grad):
        r, c = grad.shape
        return jnp.moveaxis(low(grad).reshape(2, nc // 2, r // nc, ns, c // ns), 3, 0)

    g_down = tall(mm_tn(units, top_low))
    g_gate = wide(mm_tn(normed_ffn, d_gate))
    g_up = wide(mm_tn(normed_ffn, d_up))

    def back_step(totals, x_in, x_out):
        rows_in, gain, above = x_in
        over = above[lax.axis_index("tensor")] if len(above.shape) == 3 else above[...]
        d_rows, d_gain = norm_back(rows_in[...], gain[...], totals[0])
        grad = over + d_rows
        x_out[0][...] = grad
        x_out[1][...] = d_gain
        return [low(grad)]

    ep_back = Epilogue([("tensor", shape3, BF16)], back_step)
    back_out = [sds(shape3, F32), sds((1, width), F32)]
    down_sum, cross_low_grad, cross_grad, dg_ffn = comm_(
        4,
        gathers=[], sums=[g_down], reduces=[(part_ffn, "tensor")], epilogue=ep_back,
        extra_in=[after_cross, gain_f, cot.reshape(nt, part, width)], extra_out=back_out,
    )
    cross_low_grad = cross_low_grad.reshape(rows, width)
    d_cmixed = low(mm_nt(cross_low_grad, co))
    d_cq, d_ekv = local_call(
        functools.partial(back_kernel, heads, dh, False),
        [cqs, ekv, cprobs, d_cmixed],
        [sds((rows, unit), BF16), sds((enc_span, 2 * unit), BF16)],
    )
    g_co = tall(mm_tn(cmixed, cross_low_grad))
    part_ncross = low(mm(d_cq, cq)).reshape(nt, part, width)

    def cross_back_step(totals, x_in, x_out):
        x_out[2][...] = low(totals[1])
        return back_step(totals, x_in, x_out)

    gate_sum, up_sum, co_sum, self_low_grad, self_grad, dg_cross, d_ekv_own = comm_(
        5,
        gathers=[], sums=[g_gate, g_up, g_co],
        reduces=[
            (part_ncross, "tensor"),
            (d_ekv.reshape(nc, enc_len, 2 * unit), "context"),
        ],
        epilogue=Epilogue([("tensor", shape3, BF16)], cross_back_step),
        extra_in=[after_self, gain_c, cross_grad],
        extra_out=back_out + [sds((enc_len, 2 * unit), BF16)],
    )
    self_low_grad = self_low_grad.reshape(rows, width)
    d_mixed = low(mm_nt(self_low_grad, wo))
    d_q, d_kv, diag = local_call(
        functools.partial(back_kernel, heads, dh, True),
        [q, kv, probs, d_mixed],
        [sds((rows, unit), BF16), sds((span, 2 * unit), BF16), sds((8, span), F32)],
    )

    g_wo = tall(mm_tn(mixed, self_low_grad))
    g_cq = tall(mm_tn(d_cq, normed_cross))
    g_ckv = tall(mm_tn(d_ekv_own, enc))
    part_enc = low(mm(d_ekv_own, ckv)).reshape(nt, enc_len // nt, width)

    def mid_step(totals, x_in, x_out):
        base = x_in[0][...] - x_in[1][lax.axis_index("tensor")]
        x_out[0][...] = low(totals[0])
        return [low(totals[1] + base), low(totals[2])]

    wo_sum, cq_sum, ckv_sum, out_delta, d_enc, d_kv_own = comm_(
        6,
        gathers=[], sums=[g_wo, g_cq, g_ckv],
        reduces=[
            (d_kv.reshape(nc, rows, 2 * unit), "context"),
            (part_out, "tensor"),
            (part_enc, "tensor"),
        ],
        epilogue=Epilogue(
            [("tensor", shape3, BF16), ("tensor", (enc_len // nt, width), BF16)], mid_step
        ),
        extra_in=[after_cross, x.reshape(nt, part, width)],
        extra_out=[sds((rows, 2 * unit), BF16)],
    )
    d_qkv = jnp.concatenate([d_q, d_kv_own], axis=1)
    part_nself = low(mm(d_qkv, w_qkv)).reshape(nt, part, width)
    g_self = tall(mm_tn(d_qkv, normed_self))

    bucket_d = lax.dynamic_slice(twice, (lax.rem(2 * span - ctx * rows - rows, span),), (span,))
    onehot_d = (bucket_d[None, :] == jnp.arange(bias_table.shape[0], dtype=jnp.int32)[:, None]).astype(F32)
    g_bias = lax.dot_general(
        diag, onehot_d, (((1,), (1,)), ((), ())), precision=lax.Precision.HIGHEST
    )

    def last_step(totals, x_in, x_out):
        rows_in, gain, above, cot_in, dgf, dgc = x_in
        d_rows, d_gain = norm_back(rows_in[lax.axis_index("tensor")], gain[...], totals[0])
        x_out[0][0:1, :] = dgf[...]
        x_out[0][1:2, :] = dgc[...]
        x_out[0][2:3, :] = d_gain
        x_out[0][3:8, :] = jnp.zeros_like(x_out[0][3:8, :])
        return [low(above[...] - cot_in[lax.axis_index("tensor")] + d_rows)]

    def small_fill(i, sm_in, x_out, sm_out):
        return [sm_in[0], x_out[0], sm_out[1]][i]

    gains0 = jnp.zeros((8, width), F32)
    self_sum, hid_delta, _, bias_sum, _, gain_sum = comm_(
        7,
        gathers=[], sums=[g_self], reduces=[(part_nself, "tensor")],
        epilogue=Epilogue([("tensor", shape3, BF16)], last_step, small_fill),
        extra_in=[
            x.reshape(nt, part, width), gain_s, self_grad, cot.reshape(nt, part, width),
            dg_ffn, dg_cross,
        ],
        extra_out=[sds((8, width), F32)],
        smalls=[(g_bias, "group"), (gains0, ("axis", "tensor")), (gains0, "group")],
    )

    def wide_out(total):
        return total.reshape(width // ns, total.shape[-1]).astype(F32)

    def tall_out(total):
        return total.reshape(-1, total.shape[-1]).astype(F32)

    self_w, ckv_w = tall_out(self_sum), tall_out(ckv_sum)
    return (
        (x + out_delta.reshape(rows, width).astype(F32))[None],
        (cot + hid_delta.reshape(rows, width).astype(F32))[None],
        d_enc.reshape(1, enc_len, width).astype(F32),
        gain_sum[2],
        gain_sum[1],
        gain_sum[0],
        bias_sum[:heads].T,
        self_w[:unit].T,
        self_w[unit : 2 * unit].T,
        self_w[2 * unit :].T,
        tall_out(wo_sum),
        tall_out(cq_sum).T,
        ckv_w[:unit].T,
        ckv_w[unit:].T,
        tall_out(co_sum),
        wide_out(gate_sum),
        wide_out(up_sum),
        tall_out(down_sum),
    )


def solution(mesh):
    tok = P("shard", "context", None)
    ids = P("shard", "context")
    wide, tall = P("shard", "tensor"), P("tensor", "shard")
    in_specs = (tok, tok, tok, ids, ids, ids, P("shard", None), P(), P(), P(), P(), P(None, "tensor"))
    in_specs += (wide, wide, wide, tall) * 2 + (wide, wide, tall)
    out_specs = (tok, tok, tok, P(), P(), P(), P(None, "tensor"))
    out_specs += (wide, wide, wide, tall) * 2 + (wide, wide, tall)
    sizes = {a: mesh.shape[a] for a in ("shard", "context", "tensor")}
    return jax.shard_map(
        functools.partial(body, sizes),
        mesh=mesh,
        in_specs=in_specs,
        out_specs=out_specs,
        check_vma=False,
    )
```
